32 devices in a mesh: energy: 8 (over z, core), slab: 4 (over y, x).
Axes of the slice: x: 2, y: 2, z: 4, core: 2. Of those that a mesh axis runs over, the one named last changes fastest.
Arguments:
- slab_modes: float32 [4, 512, 512], P('slab'), may hold values from -0.25 to 0.25
- levels: float32 [4, 512], P('slab'), may hold values from -2.5 to 2.5
- boundary_blocks: int32 [4, 4], P('slab'), may hold values from 0 to 7, as said below
- coupling_mask: int32 [4, 2, 2], P('slab'), may hold values from 0 to 1, as said below
- coupling: float32 [4, 128, 128], P('slab'), may hold values from -0.26516503 to 0.26516503
- phonon_shift: int32 [4], P('slab'), may hold values from 0 to 1, as said below
- prev_green: float32 [2, 4, 8, 256, 256], P(None, 'slab', 'energy'), may hold values from -1 to 0.8
Outputs:
- new_green: float32 [2, 4, 8, 512], P(None, 'slab', 'energy')
The draws below stay inside these ranges and needn't reach their ends.
Inputs may be any that keep to these rules, and one draw needn't show every extreme that they name: `boundary_blocks`: each row holds 4 different block numbers. `coupling_mask`: every row and every column of each slab's mask holds a 1. `phonon_shift`: some slab has a shift of exactly 1.
All inputs are finite; a program needn't handle non-finite values.
Results may differ from the reference program's by a relative error of at most 0.0001.
Values sent between devices are 32-bit elements; how exact they have to be, the bound alone decides.
A program may use at most 64 MiB of HBM per device.

```python
import jax
import jax.numpy as jnp
from jax import lax

ORB = 512
BLOCK = 64
NB = 2
E_DEV = 1
FACE = 128
NE = 8
SLABS = 4


def draw_boundary_blocks(key, part):
    key_list = jax.random.split(key, SLABS)
    orders = jax.vmap(lambda single: jax.random.permutation(single, ORB // BLOCK))(key_list)
    return orders[:, :2 * NB].astype(jnp.int32)


def draw_coupling_mask(key, part):
    first_key, second_key = jax.random.split(key)
    random_bits = jax.random.randint(first_key, (SLABS, NB, NB), 0, 2)
    orders = jax.vmap(lambda single: jax.random.permutation(single, NB))(jax.random.split(second_key, SLABS))
    matched = (orders[:, :, None] == jnp.arange(NB)[None, None, :]).astype(jnp.int32)
    return jnp.maximum(random_bits, matched).astype(jnp.int32)


def draw_phonon_shift(key, part):
    first_key, second_key = jax.random.split(key)
    offsets = jax.random.randint(first_key, (SLABS,), 0, E_DEV + 1)
    chosen = jax.random.randint(second_key, (), 0, SLABS)
    return jnp.where(jnp.arange(SLABS) == chosen, E_DEV, offsets).astype(jnp.int32)


def draw_prev_green(key, part):
    size_value = 2 * NB * BLOCK
    key_list = jax.random.split(key, 3)
    array_shape = (2, SLABS, NE, size_value, size_value)
    scattered = jax.random.uniform(key_list[0], array_shape, jnp.float32, -0.05, 0.05)
    diagonal_real = jax.random.uniform(key_list[1], (SLABS, NE, size_value), jnp.float32, -0.8, 0.8)
    diagonal_imag = jax.random.uniform(key_list[2], (SLABS, NE, size_value), jnp.float32, -1.0, -0.2)
    identity_matrix = jnp.eye(size_value, dtype=jnp.float32)
    diagonal = jnp.stack([diagonal_real, diagonal_imag])[..., None] * identity_matrix
    return (scattered * (1.0 - identity_matrix) + diagonal).astype(jnp.float32)


def steps_of(key, extent, shards, low, largest):
    gain, own = 1.0, jax.random.fold_in(key, 6)
    for axis_at, parts in shards:
        draws = jnp.exp(jax.random.uniform(jax.random.fold_in(own, axis_at), (parts,), jnp.float32, low / len(shards), largest / len(shards)))
        gain = gain * jnp.repeat(draws, extent[axis_at] // parts).reshape([-1 if axis == axis_at else 1 for axis in range(len(extent))])
    return gain


def scatter_about(own_key, dims, scale, bound, cuts=(), kind=jnp.bfloat16):
    gain = steps_of(own_key, dims, cuts, -0.22, 0.18) if cuts else 1.0
    entries = jax.random.normal(own_key, dims, jnp.float32) * scale * gain
    return jnp.minimum(jnp.maximum(entries, -bound), bound).astype(kind)


def setup_inputs(seed: int = 0) -> dict:
    seeds = jax.random.split(jax.random.key(seed), 8)
    return {
        "slab_modes": scatter_about(seeds[0], (SLABS, ORB, ORB), ORB ** -0.5, 0.25, ((0, 4),), jnp.float32),
        "levels": jnp.clip(jax.random.uniform(seeds[1], (SLABS, ORB), jnp.float32, -2.5, 2.5) * steps_of(seeds[1], (SLABS, ORB), ((0, 4),), -0.4, 0.0), -2.5, 2.5),
        "boundary_blocks": draw_boundary_blocks(jax.random.fold_in(seeds[7], 71), 0),
        "coupling_mask": draw_coupling_mask(jax.random.fold_in(seeds[7], 71), 0),
        "coupling": scatter_about(seeds[4], (SLABS, FACE, FACE), (1.0 / FACE ** 0.5), 0.26516503, ((0, 4),), jnp.float32),
        "phonon_shift": draw_phonon_shift(jax.random.fold_in(seeds[7], 71), 0),
        "prev_green": draw_prev_green(jax.random.fold_in(seeds[7], 71), 0),
    }


broadening = 0.2
contact_rate = 0.2
phonon_strength = 0.03
energy_low = -2.5
energy_span = 5.0
highest = lax.Precision.HIGHEST

def matmul_high(left_factor, right_factor):
    return jnp.matmul(left_factor, right_factor, precision=highest)

def complex_product(left_factor, right_factor):
    real_part = matmul_high(left_factor[0], right_factor[0]) - matmul_high(left_factor[1], right_factor[1])
    imag_part = matmul_high(left_factor[0], right_factor[1]) + matmul_high(left_factor[1], right_factor[0])
    return jnp.stack([real_part, imag_part])

def swap_last(matrix_in):
    return jnp.swapaxes(matrix_in, -1, -2)

def identity_pair(size_value):
    eye_part = jnp.eye(size_value, dtype=jnp.float32)
    return jnp.stack([eye_part, jnp.zeros_like(eye_part)])[:, None]

def solve_right(matrix, right_side):
    order_size = matrix.shape[-1]
    upper_rows = jnp.concatenate([swap_last(matrix[0]), -swap_last(matrix[1])], axis=-1)
    lower_rows = jnp.concatenate([swap_last(matrix[1]), swap_last(matrix[0])], axis=-1)
    system = jnp.concatenate([upper_rows, lower_rows], axis=-2)
    stacked = jnp.concatenate([swap_last(right_side[0]), swap_last(right_side[1])], axis=-2)
    solved = jnp.linalg.solve(system, stacked)
    return jnp.stack([swap_last(solved[..., :order_size, :]), swap_last(solved[..., order_size:, :])])

def face_rows(modes_one, blocks_one):
    pieces = []
    for number in range(2 * NB):
        start = (blocks_one[number] * BLOCK).astype(jnp.int32)
        pieces.append(lax.dynamic_slice_in_dim(modes_one, start, BLOCK, 0))
    return jnp.concatenate(pieces, axis=0)

def reference(slab_modes, levels, boundary_blocks, coupling_mask, coupling, phonon_shift, prev_green):
    energies_total = prev_green.shape[2]
    face_size = NB * BLOCK
    slab_total = slab_modes.shape[0]
    energy = energy_low + energy_span * (jnp.arange(energies_total).astype(jnp.float32) + 0.5) / energies_total
    identity_face = identity_pair(face_size)
    identity_both = identity_pair(2 * face_size)
    contact = jnp.zeros((2, energies_total, face_size, face_size), jnp.float32)
    contact = contact.at[1].set(-contact_rate * jnp.eye(face_size, dtype=jnp.float32))
    modes_all, weights_all, blocks_all, links_all = ([], [], [], [])
    for slab_number in range(slab_total):
        face_modes = face_rows(slab_modes[slab_number], boundary_blocks[slab_number])
        detuning = energy[:, None] - levels[slab_number][None, :]
        denominator = detuning * detuning + broadening * broadening
        weights = jnp.stack([detuning / denominator, -broadening / denominator])
        blocks = jnp.stack([jnp.einsum('an,en,bn->eab', face_modes, weights[0], face_modes, precision=highest), jnp.einsum('an,en,bn->eab', face_modes, weights[1], face_modes, precision=highest)])
        spread = jnp.repeat(jnp.repeat(coupling_mask[slab_number], BLOCK, axis=0), BLOCK, axis=1).astype(jnp.float32)
        modes_all.append(face_modes)
        weights_all.append(weights)
        blocks_all.append(blocks)
        links_all.append(coupling[slab_number] * spread)
    left_sigmas = []
    sigma_left = contact
    for slab_number in range(slab_total):
        left_sigmas.append(sigma_left)
        if slab_number + 1 < slab_total:
            blocks = blocks_all[slab_number]
            inner_block = blocks[:, :, :face_size, :face_size]
            resolve = solve_right(identity_face - complex_product(inner_block, sigma_left), sigma_left)
            outer_green = blocks[:, :, face_size:, face_size:] + complex_product(complex_product(blocks[:, :, face_size:, :face_size], resolve), blocks[:, :, :face_size, face_size:])
            link_matrix = links_all[slab_number]
            sigma_left = matmul_high(matmul_high(link_matrix.T, outer_green), link_matrix)
    right_sigmas = [contact for slab_number in range(slab_total)]
    sigma_right = contact
    for slab_number in range(slab_total - 1, -1, -1):
        right_sigmas[slab_number] = sigma_right
        if slab_number > 0:
            blocks = blocks_all[slab_number]
            outer_block = blocks[:, :, face_size:, face_size:]
            resolve = solve_right(identity_face - complex_product(outer_block, sigma_right), sigma_right)
            inner_green = blocks[:, :, :face_size, :face_size] + complex_product(complex_product(blocks[:, :, :face_size, face_size:], resolve), blocks[:, :, face_size:, :face_size])
            link_matrix = links_all[slab_number - 1]
            sigma_right = matmul_high(matmul_high(link_matrix, inner_green), link_matrix.T)
    results = []
    for slab_number in range(slab_total):
        padded = jnp.pad(prev_green[:, slab_number], ((0, 0), (energies_total, energies_total), (0, 0), (0, 0)))
        offset = phonon_shift[slab_number].astype(jnp.int32)
        upper_part = lax.dynamic_slice_in_dim(padded, energies_total + offset, energies_total, 1)
        lower_part = lax.dynamic_slice_in_dim(padded, energies_total - offset, energies_total, 1)
        mixing = phonon_strength * (upper_part + lower_part)
        mixing = mixing.at[:, :, :face_size, :face_size].add(left_sigmas[slab_number])
        mixing = mixing.at[:, :, face_size:, face_size:].add(right_sigmas[slab_number])
        blocks = blocks_all[slab_number]
        resolve = solve_right(identity_both - complex_product(blocks, mixing), mixing)
        face_modes = modes_all[slab_number]
        projected = matmul_high(resolve, face_modes)
        diagonal_term = jnp.sum(face_modes[None, None] * projected, axis=2)
        weights = weights_all[slab_number]
        square_real = weights[0] * weights[0] - weights[1] * weights[1]
        square_imag = 2.0 * weights[0] * weights[1]
        result_real = weights[0] + square_real * diagonal_term[0] - square_imag * diagonal_term[1]
        result_imag = weights[1] + square_real * diagonal_term[1] + square_imag * diagonal_term[0]
        results.append(jnp.stack([result_real, result_imag]))
    return jnp.stack(results, axis=1)
```

```python
import functools

import jax
import jax.numpy as jnp
from jax import lax
from jax.experimental import pallas as pl
from jax.experimental.pallas import tpu as pltpu
from jax.sharding import PartitionSpec as P

BLOCK = 64
NB = 2
FACE = BLOCK * NB

broadening = 0.2
contact_rate = 0.2
phonon_strength = 0.03
energy_low = -2.5
energy_span = 5.0
highest = lax.Precision.HIGHEST

NN = (((1,), (0,)), ((), ()))
NT = (((1,), (1,)), ((), ()))
TN = (((0,), (0,)), ((), ()))
f32 = jnp.float32
bf16 = jnp.bfloat16


def dot_full(a, b, dims=NN):
    return lax.dot_general(a, b, dims, precision=highest, preferred_element_type=f32)


def dot_fast(a, b, dims=NN):
    return lax.dot_general(a.astype(bf16), b.astype(bf16), dims, preferred_element_type=f32)


def halves(a):
    high = a.astype(bf16)
    return high, (a - high.astype(f32)).astype(bf16)


def dot_three(a, b, dims=NN):
    ah, al = halves(a)
    bh, bl = halves(b)
    dot = functools.partial(lax.dot_general, dimension_numbers=dims, preferred_element_type=f32)
    return dot(ah, bh) + (dot(ah, bl) + dot(al, bh))


def spread(y):
    m = y.shape[1] // 2
    real, imag = y[:, :m], y[:, m:]
    return jnp.concatenate(
        [jnp.concatenate([real, imag], axis=1), jnp.concatenate([-imag, real], axis=1)], axis=0
    )


def cdot(x, y, dot):
    return dot(x, spread(y))


def turned(y, sign):
    m = y.shape[1] // 2
    return jnp.concatenate([y[:, :m].T, sign * y[:, m:].T], axis=1)


def unit(n):
    rows = lax.broadcasted_iota(jnp.int32, (n, 2 * n), 0)
    columns = lax.broadcasted_iota(jnp.int32, (n, 2 * n), 1)
    return jnp.where(rows == columns, 1.0, 0.0).astype(f32)


def total(x):
    return jnp.sum(jnp.sum(x, axis=0, keepdims=True), axis=1, keepdims=True)[0, 0]


FAST_STEPS = 14
FULL_STEPS = 40


def inverse(a, x_ref, dot_last):
    n = a.shape[0]
    one = unit(n)
    adjoint = turned(a, -1.0)
    gram = cdot(a, adjoint, dot_fast)
    frobenius = jnp.sqrt(total(gram * gram))
    rows = jnp.sum(jnp.abs(gram), axis=1, keepdims=True)
    bound = jnp.minimum(frobenius, jnp.max(rows))
    scale = 1.8 / bound
    first = cdot(adjoint, 2.0 * one - scale * gram, dot_fast)
    x_ref[...] = scale * first

    def step(dot, x):
        gap = one - cdot(a, x, dot)
        x_ref[...] = cdot(x, one + gap, dot)
        return total(gap * gap)

    def fast(carry):
        count, _ = carry
        return count + 1, step(dot_fast, x_ref[...])

    def full(carry):
        count, _ = carry
        return count + 1, step(dot_last, x_ref[...])

    big = jnp.float32(1e30)
    lax.while_loop(lambda c: (c[0] < FAST_STEPS) & (c[1] > 1.0), fast, (jnp.int32(0), big))
    lax.while_loop(lambda c: (c[0] < FULL_STEPS) & (c[1] > 1e-4), full, (jnp.int32(0), big))
    return x_ref[...]


def setup_kernel(blocks_ref, energy_ref, modes_ref, levels_ref, v_ref, b_ref, w_ref):
    for number in range(2 * NB):
        start = pl.multiple_of(blocks_ref[number] * BLOCK, BLOCK)
        v_ref[number * BLOCK:(number + 1) * BLOCK, :] = modes_ref[pl.ds(start, BLOCK), :]
    detuning = energy_ref[0] - levels_ref[...]
    denominator = detuning * detuning + broadening * broadening
    real, imag = detuning / denominator, -broadening / denominator
    w_ref[...] = jnp.concatenate([real, imag], axis=0)
    v = v_ref[...]
    n = v.shape[0]
    both = dot_full(jnp.concatenate([v * real, v * imag], axis=0), v, NT)
    b_ref[...] = jnp.concatenate([both[:n], both[n:]], axis=1)


def block_of(b, row, column):
    n = b.shape[1] // 2
    part = b[row * FACE:(row + 1) * FACE]
    at = column * FACE
    return jnp.concatenate([part[:, at:at + FACE], part[:, n + at:n + at + FACE]], axis=1)


def times_real(x, y):
    m = x.shape[1] // 2
    both = dot_full(jnp.concatenate([x[:, :m], x[:, m:]], axis=0), y)
    n = x.shape[0]
    return jnp.concatenate([both[:n], both[n:]], axis=1)


def const_kernel(b_ref, here_ref, before_ref, inner_ref, arm_ref, const_ref):
    b = b_ref[...]
    ll, lr = block_of(b, 0, 0), block_of(b, 0, 1)
    rl, rr = block_of(b, 1, 0), block_of(b, 1, 1)
    here, before = here_ref[...], before_ref[...]
    inner_ref[0] = ll
    inner_ref[1] = rr
    arm_ref[0] = dot_full(here.T, rl)
    arm_ref[1] = dot_full(before, lr)
    const_ref[0] = times_real(dot_full(here.T, rr), here)
    const_ref[1] = times_real(dot_full(before, ll), before.T)


def step_kernel(meta_ref, sigma_ref, inner_ref, arm_ref, const_ref, out_ref, x_ref):
    way = meta_ref[1]

    @pl.when(meta_ref[0] == 1)
    def _():
        sigma = sigma_ref[...]
        arm = arm_ref[way]
        a = unit(FACE) - cdot(inner_ref[way], sigma, dot_full)
        early = cdot(arm, sigma, dot_full)
        x = inverse(a, x_ref, dot_full)
        out_ref[...] = const_ref[way] + cdot(cdot(early, x, dot_full), turned(arm, 1.0), dot_full)

    @pl.when(meta_ref[0] != 1)
    def _():
        out_ref[...] = jnp.zeros_like(out_ref)


def phonon_kernel(shift_ref, b_ref, own_ref, above_ref, below_ref, mix_ref, part_ref):
    shifted = shift_ref[0] != 0
    n = own_ref.shape[1]
    pieces = []
    for part in range(2):
        own = own_ref[part]
        around = jnp.where(shifted, above_ref[part] + below_ref[part], own + own)
        pieces.append(phonon_strength * around)
    mix = jnp.concatenate(pieces, axis=1)
    mix_ref[...] = mix
    part_ref[...] = unit(n) - cdot(b_ref[...], mix, dot_full)


def final_kernel(meta_ref, b_ref, v_ref, w_ref, mix_ref, part_ref, *rest):
    *incoming, out_ref, a_ref, s_ref, x_ref = rest
    slabs = len(incoming) + 1
    position = meta_ref[2]
    rows = lax.broadcasted_iota(jnp.int32, (FACE, 2 * FACE), 0)
    columns = lax.broadcasted_iota(jnp.int32, (FACE, 2 * FACE), 1)
    contact = jnp.where(columns == rows + FACE, -contact_rate, 0.0).astype(f32)
    left = jnp.where(position == 0, contact, 0.0)
    right = jnp.where(position == slabs - 1, contact, 0.0)
    for t, piece in enumerate(incoming):
        value = piece[...]
        left = jnp.where(position == t + 1, value, left)
        right = jnp.where(position == slabs - 2 - t, value, right)
    n = b_ref.shape[0]
    b = b_ref[...]
    for at, sigma in ((0, left), (FACE, right)):
        columns_of_b = jnp.concatenate([b[:, at:at + FACE], b[:, n + at:n + at + FACE]], axis=1)
        change = cdot(columns_of_b, sigma, dot_full)
        for part in range(2):
            lanes = slice(part * n + at, part * n + at + FACE)
            a_ref[:, lanes] = part_ref[:, lanes] - change[:, part * FACE:(part + 1) * FACE]
            s_ref[:, lanes] = mix_ref[:, lanes]
            s_ref[at:at + FACE, lanes] += sigma[:, part * FACE:(part + 1) * FACE]
    v = v_ref[...]
    s = s_ref[...]
    before = dot_full(s, v, TN)
    x = inverse(a_ref[...], x_ref, dot_full)
    after = dot_full(jnp.concatenate([x[:, :n], x[:, n:]], axis=0), v)
    sr, si, xr, xi = before[:n], before[n:], after[:n], after[n:]
    dr = jnp.sum(sr * xr - si * xi, axis=0, keepdims=True)
    di = jnp.sum(sr * xi + si * xr, axis=0, keepdims=True)
    wr, wi = w_ref[0:1, :], w_ref[1:2, :]
    qr, qi = wr * wr - wi * wi, 2.0 * wr * wi
    out_ref[0:1, :] = wr + qr * dr - qi * di
    out_ref[1:2, :] = wi + qr * di + qi * dr


VM = pl.BlockSpec(memory_space=pltpu.VMEM)
SM = pl.BlockSpec(memory_space=pltpu.SMEM)


def call(kernel, outs, in_specs, scratch=()):
    shapes = [jax.ShapeDtypeStruct(shape, f32) for shape in outs]
    return pl.pallas_call(
        kernel,
        out_shape=shapes,
        in_specs=in_specs,
        out_specs=[VM] * len(outs),
        scratch_shapes=[pltpu.VMEM(shape, f32) for shape in scratch],
        compiler_params=pltpu.CompilerParams(vmem_limit_bytes=48 * 1024 * 1024),
    )


def body(slab_modes, levels, boundary_blocks, coupling_mask, coupling, phonon_shift, prev_green):
    assert prev_green.shape[2] == 1
    slabs = lax.axis_size("slab")
    energies = lax.axis_size("energy")
    assert slabs % 2 == 0
    position = lax.axis_index("slab")
    grid_index = lax.axis_index("energy")
    energy = energy_low + energy_span * (grid_index.astype(f32) + 0.5) / energies
    n = 2 * FACE
    orbitals = slab_modes.shape[2]

    mask = jnp.repeat(jnp.repeat(coupling_mask[0], BLOCK, axis=0), BLOCK, axis=1).astype(f32)
    link_here = coupling[0] * mask
    link_before = lax.ppermute(link_here, "slab", [(i, i + 1) for i in range(slabs - 1)])
    own = prev_green[:, 0, 0]
    above = lax.ppermute(own, "energy", [(i + 1, i) for i in range(energies - 1)])
    below = lax.ppermute(own, "energy", [(i, i + 1) for i in range(energies - 1)])

    v, b, w = call(
        setup_kernel, [(n, orbitals), (n, 2 * n), (2, orbitals)], [SM, SM, VM, VM]
    )(boundary_blocks[0], energy[None], slab_modes[0], levels)
    pair = (2, FACE, 2 * FACE)
    inner, arm, const = call(const_kernel, [pair] * 3, [VM] * 3)(b, link_here, link_before)

    eye = jnp.eye(FACE, dtype=f32)
    sigma = jnp.concatenate([jnp.zeros_like(eye), -contact_rate * eye], axis=1)
    incoming = []
    mix = part = None
    for t in range(slabs - 1):
        active = (position == t) | (position == slabs - 1 - t)
        way = jnp.where(position == t, 0, 1)
        meta = jnp.stack([active.astype(jnp.int32), way.astype(jnp.int32), position])
        (outgoing,) = call(step_kernel, [pair[1:]], [SM] + [VM] * 4, [pair[1:]])(
            meta, sigma, inner, arm, const
        )
        sigma = lax.ppermute(
            outgoing, "slab", [(t, t + 1), (slabs - 1 - t, slabs - 2 - t)]
        )
        incoming.append(sigma)
    mix, part = call(phonon_kernel, [(n, 2 * n)] * 2, [SM] + [VM] * 4)(
        phonon_shift, b, own, above, below
    )
    (result,) = call(
        final_kernel, [(2, orbitals)], [SM] + [VM] * (5 + slabs - 1), [(n, 2 * n)] * 3
    )(meta, b, v, w, mix, part, *incoming)
    return result[:, None, None, :]


def solution(mesh):
    in_specs = (
        P("slab", None, None),
        P("slab", None),
        P("slab", None),
        P("slab", None, None),
        P("slab", None, None),
        P("slab"),
        P(None, "slab", "energy", None, None),
    )
    out_specs = P(None, "slab", "energy", None)
    return jax.shard_map(body, mesh=mesh, in_specs=in_specs, out_specs=out_specs, check_vma=False)
```

```python
import functools

import jax
import jax.numpy as jnp
from jax import lax
from jax.experimental import pallas as pl
from jax.experimental.pallas import tpu as pltpu
from jax.sharding import PartitionSpec as P

BLOCK = 64
NB = 2
FACE = BLOCK * NB

broadening = 0.2
contact_rate = 0.2
phonon_strength = 0.03
energy_low = -2.5
energy_span = 5.0

NN = (((1,), (0,)), ((), ()))
NT = (((1,), (1,)), ((), ()))
TN = (((0,), (0,)), ((), ()))
f32 = jnp.float32
bf16 = jnp.bfloat16


def dot_fast(a, b, dims=NN):
    return lax.dot_general(a.astype(bf16), b.astype(bf16), dims, preferred_element_type=f32)


def halves(a):
    high = a.astype(bf16)
    return high, (a - high.astype(f32)).astype(bf16)


def dot_three(a, b, dims=NN):
    ah, al = halves(a)
    bh, bl = halves(b)
    dot = functools.partial(lax.dot_general, dimension_numbers=dims, preferred_element_type=f32)
    return dot(ah, bh) + (dot(ah, bl) + dot(al, bh))


def spread(y):
    m = y.shape[1] // 2
    real, imag = y[:, :m], y[:, m:]
    return jnp.concatenate(
        [jnp.concatenate([real, imag], axis=1), jnp.concatenate([-imag, real], axis=1)], axis=0
    )


def cdot(x, y, dot):
    return dot(x, spread(y))


def turned(y, sign):
    m = y.shape[1] // 2
    return jnp.concatenate([y[:, :m].T, sign * y[:, m:].T], axis=1)


def unit(n):
    rows = lax.broadcasted_iota(jnp.int32, (n, 2 * n), 0)
    columns = lax.broadcasted_iota(jnp.int32, (n, 2 * n), 1)
    return jnp.where(rows == columns, 1.0, 0.0).astype(f32)


def total(x):
    return jnp.sum(jnp.sum(x, axis=0, keepdims=True), axis=1, keepdims=True)[0, 0]


FAST_STEPS = 14
FULL_STEPS = 60


def inverse(a, x_ref, dot_last):
    n = a.shape[0]
    one = unit(n)
    adjoint = turned(a, -1.0)
    gram = cdot(a, adjoint, dot_fast)
    frobenius = jnp.sqrt(total(gram * gram))
    rows = jnp.sum(jnp.abs(gram), axis=1, keepdims=True)
    bound = jnp.minimum(frobenius, jnp.max(rows))
    scale = 1.8 / bound
    first = cdot(adjoint, 2.0 * one - scale * gram, dot_fast)
    x_ref[...] = scale * first

    def step(dot, x):
        gap = one - cdot(a, x, dot)
        x_ref[...] = cdot(x, one + gap, dot)
        return total(gap * gap)

    def fast(carry):
        count, _ = carry
        return count + 1, step(dot_fast, x_ref[...])

    def full(carry):
        count, _ = carry
        return count + 1, step(dot_last, x_ref[...])

    big = jnp.float32(1e30)
    lax.while_loop(lambda c: (c[0] < FAST_STEPS) & (c[1] > 1.0), fast, (jnp.int32(0), big))
    lax.while_loop(lambda c: (c[0] < FULL_STEPS) & (c[1] > 1e-4), full, (jnp.int32(0), big))
    return x_ref[...]


def block_of(b, row, column):
    n = b.shape[1] // 2
    part = b[row * FACE:(row + 1) * FACE]
    at = column * FACE
    return jnp.concatenate([part[:, at:at + FACE], part[:, n + at:n + at + FACE]], axis=1)


def times_real(x, y):
    m = x.shape[1] // 2
    both = dot_three(jnp.concatenate([x[:, :m], x[:, m:]], axis=0), y)
    n = x.shape[0]
    return jnp.concatenate([both[:n], both[n:]], axis=1)


def setup_kernel(
    blocks_ref, mask_ref, last_ref, energy_ref, modes_ref, levels_ref, coupling_ref,
    link_ref, v_ref, b_ref, w_ref, inner_ref, arm_ref, const_ref, sems,
):
    copies = []
    for number in range(2 * NB):
        start = pl.multiple_of(blocks_ref[number] * BLOCK, BLOCK)
        copies.append(
            pltpu.make_async_copy(
                modes_ref.at[pl.ds(start, BLOCK), :],
                v_ref.at[pl.ds(number * BLOCK, BLOCK), :],
                sems.at[number],
            )
        )
        copies[-1].start()
    detuning = energy_ref[0] - levels_ref[...]
    denominator = detuning * detuning + broadening * broadening
    real, imag = detuning / denominator, -broadening / denominator
    w_ref[...] = jnp.concatenate([real, imag], axis=0)
    for copy in copies:
        copy.wait()
    v = v_ref[...]
    n = v.shape[0]
    both = dot_three(jnp.concatenate([v * real, v * imag], axis=0), v, NT)
    b_ref[...] = jnp.concatenate([both[:n], both[n:]], axis=1)
    b = b_ref[...]
    ll, lr = block_of(b, 0, 0), block_of(b, 0, 1)
    rl, rr = block_of(b, 1, 0), block_of(b, 1, 1)
    rows = lax.broadcasted_iota(jnp.int32, (FACE, FACE), 0)
    columns = lax.broadcasted_iota(jnp.int32, (FACE, FACE), 1)
    ones = [[mask_ref[i, j].astype(f32) for j in range(NB)] for i in range(NB)]
    upper = jnp.where(columns < BLOCK, ones[0][0], ones[0][1])
    lower = jnp.where(columns < BLOCK, ones[1][0], ones[1][1])
    masked = coupling_ref[...] * jnp.where(rows < BLOCK, upper, lower)
    link = jnp.where(last_ref[0] == 1, jnp.where(rows == columns, 1.0, 0.0), masked)
    link_ref[...] = link
    coupled = times_real(dot_three(link.T, rr), link)
    inner_ref[0] = ll
    inner_ref[1] = coupled
    arm_ref[0] = dot_three(link.T, rl)
    arm_ref[1] = times_real(lr, link)
    const_ref[0] = coupled
    const_ref[1] = ll


def contact_sigma():
    rows = lax.broadcasted_iota(jnp.int32, (FACE, 2 * FACE), 0)
    columns = lax.broadcasted_iota(jnp.int32, (FACE, 2 * FACE), 1)
    return jnp.where(columns == rows + FACE, -contact_rate, 0.0).astype(f32)


def initial_kernel(meta_ref, inner_ref, arm_ref, const_ref, out_ref, x_ref):
    one_step(meta_ref, contact_sigma, inner_ref, arm_ref, const_ref, out_ref, x_ref)


def step_kernel(meta_ref, sigma_ref, order_ref, inner_ref, arm_ref, const_ref, out_ref, x_ref):
    del order_ref
    one_step(meta_ref, lambda: sigma_ref[...], inner_ref, arm_ref, const_ref, out_ref, x_ref)


def one_step(meta_ref, sigma_of, inner_ref, arm_ref, const_ref, out_ref, x_ref):
    way = meta_ref[1]

    @pl.when(meta_ref[0] == 1)
    def _():
        sigma = sigma_of()
        arm = arm_ref[way]
        a = unit(FACE) - cdot(inner_ref[way], sigma, dot_three)
        early = cdot(arm, sigma, dot_three)
        x = inverse(a, x_ref, dot_three)
        out_ref[...] = const_ref[way] + cdot(cdot(early, x, dot_three), turned(arm, 1.0), dot_three)

    @pl.when(meta_ref[0] != 1)
    def _():
        out_ref[...] = jnp.zeros_like(out_ref)


def phonon_kernel(
    shift_ref, b_ref, own_ref, order_ref, mix_ref, part_ref, above_ref, below_ref, sent, came
):
    del order_ref
    here, energies = lax.axis_index("energy"), lax.axis_size("energy")
    has_above, has_below = here < energies - 1, here > 0
    up, down = {"energy": here + 1}, {"energy": here - 1}
    mesh = pl.DeviceIdType.MESH
    barrier = pltpu.get_barrier_semaphore()

    @pl.when(has_above)
    def _():
        pl.semaphore_signal(barrier, inc=1, device_id=up, device_id_type=mesh)

    @pl.when(has_below)
    def _():
        pl.semaphore_signal(barrier, inc=1, device_id=down, device_id_type=mesh)

    pl.semaphore_wait(barrier, has_above.astype(jnp.int32) + has_below.astype(jnp.int32))

    to_above = pltpu.make_async_remote_copy(
        own_ref, below_ref, sent.at[0], came.at[0], device_id=up, device_id_type=mesh
    )
    to_below = pltpu.make_async_remote_copy(
        own_ref, above_ref, sent.at[1], came.at[1], device_id=down, device_id_type=mesh
    )

    @pl.when(has_above)
    def _():
        to_above.start()

    @pl.when(has_below)
    def _():
        to_below.start()

    @pl.when(has_below)
    def _():
        to_above.wait_recv()
        to_below.wait_send()

    @pl.when(has_above)
    def _():
        to_below.wait_recv()
        to_above.wait_send()

    @pl.when(jnp.logical_not(has_below))
    def _():
        below_ref[...] = jnp.zeros_like(below_ref)

    @pl.when(jnp.logical_not(has_above))
    def _():
        above_ref[...] = jnp.zeros_like(above_ref)

    shifted = shift_ref[0] != 0
    n = own_ref.shape[1]
    pieces = []
    for part in range(2):
        own = own_ref[part]
        around = jnp.where(shifted, above_ref[part] + below_ref[part], own + own)
        pieces.append(phonon_strength * around)
    mix = jnp.concatenate(pieces, axis=1)
    mix_ref[...] = mix
    part_ref[...] = unit(n) - cdot(b_ref[...], mix, dot_three)


def final_kernel(meta_ref, link_ref, b_ref, v_ref, w_ref, mix_ref, part_ref, *rest):
    *incoming, out_ref, a_ref, s_ref, x_ref = rest
    slabs = len(incoming) + 1
    position = meta_ref[2]
    contact = contact_sigma()
    left = jnp.where(position == 0, contact, 0.0)
    right = jnp.where(position == slabs - 1, contact, 0.0)
    for t, piece in enumerate(incoming):
        value = piece[...]
        left = jnp.where(position == t + 1, value, left)
        right = jnp.where(position == slabs - 2 - t, value, right)
    link = link_ref[...]
    right = times_real(dot_three(link, right), link.T)
    n = b_ref.shape[0]
    b = b_ref[...]
    for at, sigma in ((0, left), (FACE, right)):
        columns_of_b = jnp.concatenate([b[:, at:at + FACE], b[:, n + at:n + at + FACE]], axis=1)
        change = cdot(columns_of_b, sigma, dot_three)
        for part in range(2):
            lanes = slice(part * n + at, part * n + at + FACE)
            a_ref[:, lanes] = part_ref[:, lanes] - change[:, part * FACE:(part + 1) * FACE]
            s_ref[:, lanes] = mix_ref[:, lanes]
            s_ref[at:at + FACE, lanes] += sigma[:, part * FACE:(part + 1) * FACE]
    v = v_ref[...]
    s = s_ref[...]
    before = dot_three(s, v, TN)
    x = inverse(a_ref[...], x_ref, dot_three)
    after = dot_three(jnp.concatenate([x[:, :n], x[:, n:]], axis=0), v)
    sr, si, xr, xi = before[:n], before[n:], after[:n], after[n:]
    dr = jnp.sum(sr * xr - si * xi, axis=0, keepdims=True)
    di = jnp.sum(sr * xi + si * xr, axis=0, keepdims=True)
    wr, wi = w_ref[0:1, :], w_ref[1:2, :]
    qr, qi = wr * wr - wi * wi, 2.0 * wr * wi
    out_ref[0, 0] = wr + qr * dr - qi * di
    out_ref[1, 0] = wi + qr * di + qi * dr


VM = pl.BlockSpec(memory_space=pltpu.VMEM)
SM = pl.BlockSpec(memory_space=pltpu.SMEM)
ANY = pl.BlockSpec(memory_space=pl.ANY)
HB = pl.BlockSpec(memory_space=pltpu.HBM)


def call(kernel, outs, in_specs, scratch=()):
    shapes = [jax.ShapeDtypeStruct(shape, f32) for shape in outs]
    return pl.pallas_call(
        kernel,
        out_shape=shapes,
        in_specs=in_specs,
        out_specs=[VM] * len(outs),
        scratch_shapes=[pltpu.VMEM(x, f32) if isinstance(x, tuple) else x for x in scratch],
        compiler_params=pltpu.CompilerParams(vmem_limit_bytes=48 * 1024 * 1024),
    )


def body(slab_modes, levels, boundary_blocks, coupling_mask, coupling, phonon_shift, prev_green):
    assert prev_green.shape[2] == 1
    slabs = lax.axis_size("slab")
    energies = lax.axis_size("energy")
    assert slabs % 2 == 0
    position = lax.axis_index("slab")
    grid_index = lax.axis_index("energy")
    energy = energy_low + energy_span * (grid_index.astype(f32) + 0.5) / energies
    n = 2 * FACE
    orbitals = slab_modes.shape[2]

    pair = (2, FACE, 2 * FACE)
    last = (position == slabs - 1).astype(jnp.int32)[None]
    link, v, b, w, inner, arm, const = call(
        setup_kernel,
        [(FACE, FACE), (n, orbitals), (n, 2 * n), (2, orbitals), pair, pair, pair],
        [SM] * 4 + [HB, VM, VM],
        [pltpu.SemaphoreType.DMA((2 * NB,))],
    )(
        boundary_blocks[0], coupling_mask[0], last, energy[None],
        slab_modes[0], levels, coupling[0],
    )

    sigma = mix = part = None
    incoming = []
    buffer = pltpu.VMEM((2, n, n), f32)
    for t in range(slabs - 1):
        active = (position == t) | (position == slabs - 1 - t)
        way = jnp.where(position == t, 0, 1)
        meta = jnp.stack([active.astype(jnp.int32), way.astype(jnp.int32), position])
        kernel, given, specs = initial_kernel, (), []
        if t:
            kernel, given, specs = step_kernel, (sigma, mix), [VM, ANY]
        (outgoing,) = call(kernel, [pair[1:]], [SM] + specs + [VM] * 3, [pair[1:]])(
            meta, *given, inner, arm, const
        )
        sigma = lax.ppermute(
            outgoing, "slab", [(t, t + 1), (slabs - 1 - t, slabs - 2 - t)]
        )
        incoming.append(sigma)
        if t == 0:
            mix, part = pl.pallas_call(
                phonon_kernel,
                out_shape=[jax.ShapeDtypeStruct((n, 2 * n), f32)] * 2,
                in_specs=[SM, VM, VM, ANY],
                out_specs=[VM, VM],
                scratch_shapes=[
                    buffer, buffer, pltpu.SemaphoreType.DMA((2,)), pltpu.SemaphoreType.DMA((2,)),
                ],
                cost_estimate=pl.CostEstimate(
                    flops=2 * 10**8, bytes_accessed=3 * 10**7, transcendentals=0
                ),
                compiler_params=pltpu.CompilerParams(
                    collective_id=0, has_side_effects=True, vmem_limit_bytes=48 * 1024 * 1024
                ),
            )(phonon_shift, b, prev_green[:, 0, 0], outgoing)
    (result,) = call(
        final_kernel, [(2, 1, 1, orbitals)], [SM] + [VM] * (6 + slabs - 1), [(n, 2 * n)] * 3
    )(meta, link, b, v, w, mix, part, *incoming)
    return result


def solution(mesh):
    in_specs = (
        P("slab", None, None),
        P("slab", None),
        P("slab", None),
        P("slab", None, None),
        P("slab", None, None),
        P("slab"),
        P(None, "slab", "energy", None, None),
    )
    out_specs = P(None, "slab", "energy", None)
    return jax.shard_map(body, mesh=mesh, in_specs=in_specs, out_specs=out_specs, check_vma=False)
```

```python
import functools

import jax
import jax.numpy as jnp
from jax import lax
from jax.experimental import pallas as pl
from jax.experimental.pallas import tpu as pltpu
from jax.sharding import PartitionSpec as P

BLOCK = 64
NB = 2
FACE = BLOCK * NB

broadening = 0.2
contact_rate = 0.2
phonon_strength = 0.03
energy_low = -2.5
energy_span = 5.0

NN = (((1,), (0,)), ((), ()))
NT = (((1,), (1,)), ((), ()))
TN = (((0,), (0,)), ((), ()))
f32 = jnp.float32
bf16 = jnp.bfloat16


def dot_fast(a, b, dims=NN):
    return lax.dot_general(a.astype(bf16), b.astype(bf16), dims, preferred_element_type=f32)


def halves(a):
    high = a.astype(bf16)
    return high, (a - high.astype(f32)).astype(bf16)


def dot_three(a, b, dims=NN):
    ah, al = halves(a)
    bh, bl = halves(b)
    dot = functools.partial(lax.dot_general, dimension_numbers=dims, preferred_element_type=f32)
    return dot(ah, bh) + (dot(ah, bl) + dot(al, bh))


def spread(y):
    m = y.shape[1] // 2
    real, imag = y[:, :m], y[:, m:]
    return jnp.concatenate(
        [jnp.concatenate([real, imag], axis=1), jnp.concatenate([-imag, real], axis=1)], axis=0
    )


def cdot(x, y, dot):
    return dot(x, spread(y))


def turned(y, sign):
    m = y.shape[1] // 2
    return jnp.concatenate([y[:, :m].T, sign * y[:, m:].T], axis=1)


def unit(n):
    rows = lax.broadcasted_iota(jnp.int32, (n, 2 * n), 0)
    columns = lax.broadcasted_iota(jnp.int32, (n, 2 * n), 1)
    return jnp.where(rows == columns, 1.0, 0.0).astype(f32)


def total(x):
    return jnp.sum(jnp.sum(x, axis=0, keepdims=True), axis=1, keepdims=True)[0, 0]


FAST_STEPS = 14
FULL_STEPS = 40


def inverse(a, x_ref):
    n = a.shape[0]
    one = unit(n)
    adjoint = turned(a, -1.0)
    high, low = halves(a)
    dot = functools.partial(lax.dot_general, dimension_numbers=NN, preferred_element_type=f32)

    def cfast(x, y):
        return dot(x.astype(bf16), spread(y.astype(bf16)))

    gram = cfast(high, adjoint)
    frobenius = jnp.sqrt(total(gram * gram))
    rows = jnp.sum(jnp.abs(gram), axis=1, keepdims=True)
    bound = jnp.minimum(frobenius, jnp.max(rows))
    scale = 1.8 / bound
    x_ref[...] = scale * cfast(adjoint, 2.0 * one - scale * gram)

    def gap_of(x):
        xh, xl = halves(x)
        sh, sl = spread(xh), spread(xl)
        return one - (dot(high, sh) + (dot(high, sl) + dot(low, sh)))

    def fast(carry):
        count, _ = carry
        x = x_ref[...]
        gap = one - cfast(high, x)
        x_ref[...] = cfast(x, one + gap)
        return count + 1, total(gap * gap)

    def slow(carry):
        count, _ = carry
        x = x_ref[...]
        gap = gap_of(x)
        x_ref[...] = cdot(x, one + gap, dot_three)
        return count + 1, total(gap * gap)

    def refine(carry):
        count, _ = carry
        x = x_ref[...]
        gap = gap_of(x)
        x_ref[...] = x + cfast(x, gap)
        return count + 1, total(gap * gap)

    state = (jnp.int32(0), jnp.float32(1e30))
    state = lax.while_loop(lambda c: (c[0] < FAST_STEPS) & (c[1] > 1.0), fast, state)
    state = lax.while_loop(lambda c: (c[0] < FULL_STEPS) & (c[1] > 1.0), slow, state)
    state = (state[0], jnp.float32(1e30))
    lax.while_loop(lambda c: (c[0] < 2 * FULL_STEPS) & (c[1] > 1e-4), refine, state)
    return x_ref[...]


def block_of(b, row, column):
    n = b.shape[1] // 2
    part = b[row * FACE:(row + 1) * FACE]
    at = column * FACE
    return jnp.concatenate([part[:, at:at + FACE], part[:, n + at:n + at + FACE]], axis=1)


def times_real(x, y):
    m = x.shape[1] // 2
    both = dot_three(jnp.concatenate([x[:, :m], x[:, m:]], axis=0), y)
    n = x.shape[0]
    return jnp.concatenate([both[:n], both[n:]], axis=1)


def setup_kernel(
    blocks_ref, mask_ref, last_ref, energy_ref, modes_ref, levels_ref, coupling_ref,
    link_ref, v_ref, b_ref, w_ref, inner_ref, arm_ref, const_ref, sems,
):
    copies = []
    for number in range(2 * NB):
        start = pl.multiple_of(blocks_ref[number] * BLOCK, BLOCK)
        copies.append(
            pltpu.make_async_copy(
                modes_ref.at[pl.ds(start, BLOCK), :],
                v_ref.at[pl.ds(number * BLOCK, BLOCK), :],
                sems.at[number],
            )
        )
        copies[-1].start()
    detuning = energy_ref[0] - levels_ref[...]
    denominator = detuning * detuning + broadening * broadening
    real, imag = detuning / denominator, -broadening / denominator
    w_ref[...] = jnp.concatenate([real, imag], axis=0)
    for copy in copies:
        copy.wait()
    v = v_ref[...]
    n = v.shape[0]
    both = dot_three(jnp.concatenate([v * real, v * imag], axis=0), v, NT)
    b_ref[...] = jnp.concatenate([both[:n], both[n:]], axis=1)
    b = b_ref[...]
    ll, lr = block_of(b, 0, 0), block_of(b, 0, 1)
    rl, rr = block_of(b, 1, 0), block_of(b, 1, 1)
    rows = lax.broadcasted_iota(jnp.int32, (FACE, FACE), 0)
    columns = lax.broadcasted_iota(jnp.int32, (FACE, FACE), 1)
    ones = [[mask_ref[i, j].astype(f32) for j in range(NB)] for i in range(NB)]
    upper = jnp.where(columns < BLOCK, ones[0][0], ones[0][1])
    lower = jnp.where(columns < BLOCK, ones[1][0], ones[1][1])
    masked = coupling_ref[...] * jnp.where(rows < BLOCK, upper, lower)
    link = jnp.where(last_ref[0] == 1, jnp.where(rows == columns, 1.0, 0.0), masked)
    link_ref[...] = link
    coupled = times_real(dot_three(link.T, rr), link)
    inner_ref[0] = ll
    inner_ref[1] = coupled
    arm_ref[0] = dot_three(link.T, rl)
    arm_ref[1] = times_real(lr, link)
    const_ref[0] = coupled
    const_ref[1] = ll


def contact_sigma():
    rows = lax.broadcasted_iota(jnp.int32, (FACE, 2 * FACE), 0)
    columns = lax.broadcasted_iota(jnp.int32, (FACE, 2 * FACE), 1)
    return jnp.where(columns == rows + FACE, -contact_rate, 0.0).astype(f32)


def initial_kernel(meta_ref, inner_ref, arm_ref, const_ref, out_ref, x_ref):
    one_step(meta_ref, contact_sigma, inner_ref, arm_ref, const_ref, out_ref, x_ref)


def step_kernel(meta_ref, sigma_ref, inner_ref, arm_ref, const_ref, out_ref, x_ref):
    one_step(meta_ref, lambda: sigma_ref[...], inner_ref, arm_ref, const_ref, out_ref, x_ref)


def one_step(meta_ref, sigma_of, inner_ref, arm_ref, const_ref, out_ref, x_ref):
    way = meta_ref[1]

    @pl.when(meta_ref[0] == 1)
    def _():
        sigma = sigma_of()
        arm = arm_ref[way]
        a = unit(FACE) - cdot(inner_ref[way], sigma, dot_three)
        early = cdot(arm, sigma, dot_three)
        x = inverse(a, x_ref)
        out_ref[...] = const_ref[way] + cdot(cdot(early, x, dot_three), turned(arm, 1.0), dot_three)


MESH = pl.DeviceIdType.MESH


class Hop:
    def __init__(self, t, out_ref, in_ref, sent, came):
        here, slabs = lax.axis_index("slab"), lax.axis_size("slab")
        self.sides = []
        for side, (start, end) in enumerate(((t, t + 1), (slabs - 1 - t, slabs - 2 - t))):
            copy = pltpu.make_async_remote_copy(
                out_ref, in_ref, sent.at[side], came.at[side],
                device_id={"slab": end}, device_id_type=MESH,
            )
            self.sides.append((here == start, here == end, start, copy))

    def greet(self, barrier):
        for _, receives, start, _ in self.sides:
            @pl.when(receives)
            def _():
                pl.semaphore_signal(barrier, inc=1, device_id={"slab": start}, device_id_type=MESH)

    def expected(self):
        return sum(sends.astype(jnp.int32) for sends, _, _, _ in self.sides)

    def start(self):
        for sends, _, _, copy in self.sides:
            @pl.when(sends)
            def _():
                copy.start()

    def wait(self):
        for sends, receives, _, copy in self.sides:
            @pl.when(sends)
            def _():
                copy.wait_send()

            @pl.when(receives)
            def _():
                copy.wait_recv()


class Halo:
    def __init__(self, own_ref, above_ref, below_ref, first, count, sent, came):
        here, energies = lax.axis_index("energy"), lax.axis_size("energy")
        self.has_above, self.has_below = here < energies - 1, here > 0
        self.up, self.down = {"energy": here + 1}, {"energy": here - 1}
        rows = pl.ds(first, count)
        own = own_ref.at[:, rows, :]
        self.to_above = pltpu.make_async_remote_copy(
            own, below_ref, sent.at[0], came.at[0], device_id=self.up, device_id_type=MESH
        )
        self.to_below = pltpu.make_async_remote_copy(
            own, above_ref, sent.at[1], came.at[1], device_id=self.down, device_id_type=MESH
        )
        self.landing = (above_ref, below_ref)

    def greet(self, barrier):
        for there, device in ((self.has_above, self.up), (self.has_below, self.down)):
            @pl.when(there)
            def _():
                pl.semaphore_signal(barrier, inc=1, device_id=device, device_id_type=MESH)

    def expected(self):
        return self.has_above.astype(jnp.int32) + self.has_below.astype(jnp.int32)

    def start(self):
        above_ref, below_ref = self.landing

        @pl.when(self.has_above)
        def _():
            self.to_above.start()

        @pl.when(self.has_below)
        def _():
            self.to_below.start()

        @pl.when(jnp.logical_not(self.has_below))
        def _():
            below_ref[...] = jnp.zeros_like(below_ref)

        @pl.when(jnp.logical_not(self.has_above))
        def _():
            above_ref[...] = jnp.zeros_like(above_ref)

    def wait(self):
        @pl.when(self.has_below)
        def _():
            self.to_above.wait_recv()
            self.to_below.wait_send()

        @pl.when(self.has_above)
        def _():
            self.to_below.wait_recv()
            self.to_above.wait_send()


def open_all(parts):
    barrier = pltpu.get_barrier_semaphore()
    for part in parts:
        part.greet(barrier)
    expected = sum(part.expected() for part in parts)

    @pl.when(expected > 0)
    def _():
        pl.semaphore_wait(barrier, expected)


EARLY_ROWS = 192


def first_hop(t, out_ref, own_ref, in_ref, above_ref, below_ref, s0, c0, s1, c1):
    hop = Hop(t, out_ref, in_ref, s0, c0)
    halo = Halo(own_ref, above_ref, below_ref, 0, EARLY_ROWS, s1, c1)
    open_all([hop, halo])
    hop.start()
    halo.start()
    halo.wait()
    hop.wait()


def middle_hop(t, out_ref, in_ref, s0, c0):
    hop = Hop(t, out_ref, in_ref, s0, c0)
    open_all([hop])
    hop.start()
    hop.wait()


def last_hop(
    t, shift_ref, out_ref, own_ref, b_ref, above_ref, below_ref,
    in_ref, mix_ref, part_ref, above_rest, below_rest, s0, c0, s1, c1,
):
    n = own_ref.shape[1]
    hop = Hop(t, out_ref, in_ref, s0, c0)
    halo = Halo(own_ref, above_rest, below_rest, EARLY_ROWS, n - EARLY_ROWS, s1, c1)
    open_all([hop, halo])
    hop.start()
    halo.start()
    shifted = shift_ref[0] != 0

    def mix_rows(rows, above, below):
        for part in range(2):
            own = own_ref[part, rows, :]
            around = jnp.where(shifted, above[part] + below[part], own + own)
            mix_ref[rows, part * n:(part + 1) * n] = phonon_strength * around

    mix_rows(slice(0, EARLY_ROWS), above_ref, below_ref)
    halo.wait()
    mix_rows(slice(EARLY_ROWS, n), above_rest, below_rest)
    part_ref[...] = unit(n) - cdot(b_ref[...], mix_ref[...], dot_three)
    hop.wait()


def final_kernel(meta_ref, link_ref, b_ref, v_ref, w_ref, mix_ref, part_ref, *rest):
    *incoming, out_ref, a_ref, s_ref, x_ref = rest
    slabs = len(incoming) + 1
    position = meta_ref[2]
    contact = contact_sigma()
    left = jnp.where(position == 0, contact, 0.0)
    right = jnp.where(position == slabs - 1, contact, 0.0)
    for t, piece in enumerate(incoming):
        value = piece[...]
        left = jnp.where(position == t + 1, value, left)
        right = jnp.where(position == slabs - 2 - t, value, right)
    link = link_ref[...]
    right = times_real(dot_three(link, right), link.T)
    n = b_ref.shape[0]
    b = b_ref[...]
    for at, sigma in ((0, left), (FACE, right)):
        columns_of_b = jnp.concatenate([b[:, at:at + FACE], b[:, n + at:n + at + FACE]], axis=1)
        change = cdot(columns_of_b, sigma, dot_three)
        for part in range(2):
            lanes = slice(part * n + at, part * n + at + FACE)
            a_ref[:, lanes] = part_ref[:, lanes] - change[:, part * FACE:(part + 1) * FACE]
            s_ref[:, lanes] = mix_ref[:, lanes]
            s_ref[at:at + FACE, lanes] += sigma[:, part * FACE:(part + 1) * FACE]
    v = v_ref[...]
    s = s_ref[...]
    before = dot_three(s, v, TN)
    x = inverse(a_ref[...], x_ref)
    after = dot_three(jnp.concatenate([x[:, :n], x[:, n:]], axis=0), v)
    sr, si, xr, xi = before[:n], before[n:], after[:n], after[n:]
    dr = jnp.sum(sr * xr - si * xi, axis=0, keepdims=True)
    di = jnp.sum(sr * xi + si * xr, axis=0, keepdims=True)
    wr, wi = w_ref[0:1, :], w_ref[1:2, :]
    qr, qi = wr * wr - wi * wi, 2.0 * wr * wi
    out_ref[0, 0] = wr + qr * dr - qi * di
    out_ref[1, 0] = wi + qr * di + qi * dr


VM = pl.BlockSpec(memory_space=pltpu.VMEM)
SM = pl.BlockSpec(memory_space=pltpu.SMEM)
ANY = pl.BlockSpec(memory_space=pl.ANY)
HB = pl.BlockSpec(memory_space=pltpu.HBM)


def call(kernel, outs, in_specs, scratch=(), channel=None):
    shapes = [jax.ShapeDtypeStruct(shape, f32) for shape in outs]
    return pl.pallas_call(
        kernel,
        out_shape=shapes,
        in_specs=in_specs,
        out_specs=[VM] * len(outs),
        scratch_shapes=[pltpu.VMEM(x, f32) if isinstance(x, tuple) else x for x in scratch],
        compiler_params=pltpu.CompilerParams(
            vmem_limit_bytes=48 * 1024 * 1024,
            collective_id=channel,
            has_side_effects=channel is not None,
        ),
    )


def body(slab_modes, levels, boundary_blocks, coupling_mask, coupling, phonon_shift, prev_green):
    assert prev_green.shape[2] == 1
    slabs = lax.axis_size("slab")
    energies = lax.axis_size("energy")
    assert slabs % 2 == 0
    position = lax.axis_index("slab")
    grid_index = lax.axis_index("energy")
    energy = energy_low + energy_span * (grid_index.astype(f32) + 0.5) / energies
    n = 2 * FACE
    orbitals = slab_modes.shape[2]

    pair = (2, FACE, 2 * FACE)
    last = (position == slabs - 1).astype(jnp.int32)[None]
    link, v, b, w, inner, arm, const = call(
        setup_kernel,
        [(FACE, FACE), (n, orbitals), (n, 2 * n), (2, orbitals), pair, pair, pair],
        [SM] * 4 + [HB, VM, VM],
        [pltpu.SemaphoreType.DMA((2 * NB,))],
    )(
        boundary_blocks[0], coupling_mask[0], last, energy[None],
        slab_modes[0], levels, coupling[0],
    )

    sigma = mix = part = None
    incoming = []
    own = prev_green[:, 0, 0]
    early = (2, EARLY_ROWS, n)
    rest = pltpu.VMEM((2, n - EARLY_ROWS, n), f32)
    two = pltpu.SemaphoreType.DMA((2,))
    assert slabs >= 4
    for t in range(slabs - 1):
        active = (position == t) | (position == slabs - 1 - t)
        way = jnp.where(position == t, 0, 1)
        meta = jnp.stack([active.astype(jnp.int32), way.astype(jnp.int32), position])
        kernel, given = (step_kernel, (sigma,)) if t else (initial_kernel, ())
        (outgoing,) = call(kernel, [pair[1:]], [SM] + [VM] * (3 + len(given)), [pair[1:]])(
            meta, *given, inner, arm, const
        )
        if t == 0:
            sigma, above, below = call(
                functools.partial(first_hop, t), [pair[1:], early, early], [VM] * 2,
                [two] * 4, t,
            )(outgoing, own)
        elif t < slabs - 2:
            (sigma,) = call(
                functools.partial(middle_hop, t), [pair[1:]], [VM], [two] * 2, t
            )(outgoing)
        else:
            sigma, mix, part = call(
                functools.partial(last_hop, t), [pair[1:], (n, 2 * n), (n, 2 * n)],
                [SM] + [VM] * 5, [rest, rest] + [two] * 4, t,
            )(phonon_shift, outgoing, own, b, above, below)
        incoming.append(sigma)
    (result,) = call(
        final_kernel, [(2, 1, 1, orbitals)], [SM] + [VM] * (6 + slabs - 1), [(n, 2 * n)] * 3
    )(meta, link, b, v, w, mix, part, *incoming)
    return result


def solution(mesh):
    in_specs = (
        P("slab", None, None),
        P("slab", None),
        P("slab", None),
        P("slab", None, None),
        P("slab", None, None),
        P("slab"),
        P(None, "slab", "energy", None, None),
    )
    out_specs = P(None, "slab", "energy", None)
    return jax.shard_map(body, mesh=mesh, in_specs=in_specs, out_specs=out_specs, check_vma=False)
```

```python
import functools

import jax
import jax.numpy as jnp
from jax import lax
from jax.experimental import pallas as pl
from jax.experimental.pallas import tpu as pltpu
from jax.sharding import PartitionSpec as P

BLOCK = 64
NB = 2
FACE = BLOCK * NB

broadening = 0.2
contact_rate = 0.2
phonon_strength = 0.03
energy_low = -2.5
energy_span = 5.0

NN = (((1,), (0,)), ((), ()))
NT = (((1,), (1,)), ((), ()))
TN = (((0,), (0,)), ((), ()))
f32 = jnp.float32
bf16 = jnp.bfloat16


def dot_fast(a, b, dims=NN):
    return lax.dot_general(a.astype(bf16), b.astype(bf16), dims, preferred_element_type=f32)


def halves(a):
    high = a.astype(bf16)
    return high, (a - high.astype(f32)).astype(bf16)


def dot_three(a, b, dims=NN):
    ah, al = halves(a)
    bh, bl = halves(b)
    dot = functools.partial(lax.dot_general, dimension_numbers=dims, preferred_element_type=f32)
    return dot(ah, bh) + (dot(ah, bl) + dot(al, bh))


def spread(y):
    m = y.shape[1] // 2
    real, imag = y[:, :m], y[:, m:]
    return jnp.concatenate(
        [jnp.concatenate([real, imag], axis=1), jnp.concatenate([-imag, real], axis=1)], axis=0
    )


def cdot(x, y, dot):
    return dot(x, spread(y))


def turned(y, sign):
    m = y.shape[1] // 2
    return jnp.concatenate([y[:, :m].T, sign * y[:, m:].T], axis=1)


def unit(n):
    rows = lax.broadcasted_iota(jnp.int32, (n, 2 * n), 0)
    columns = lax.broadcasted_iota(jnp.int32, (n, 2 * n), 1)
    return jnp.where(rows == columns, 1.0, 0.0).astype(f32)


def total(x):
    return jnp.sum(jnp.sum(x, axis=0, keepdims=True), axis=1, keepdims=True)[0, 0]


BOOST = 1.85
FAST_STEPS = 14
FULL_STEPS = 40


def inverse(a, x_ref, boosts):
    n = a.shape[0]
    one = unit(n)
    adjoint = turned(a, -1.0)
    high, low = halves(a)
    dot = functools.partial(lax.dot_general, dimension_numbers=NN, preferred_element_type=f32)

    def cfast(x, y):
        return dot(x.astype(bf16), spread(y.astype(bf16)))

    gram = cfast(high, adjoint)
    frobenius = jnp.sqrt(total(gram * gram))
    rows = jnp.sum(jnp.abs(gram), axis=1, keepdims=True)
    bound = jnp.minimum(frobenius, jnp.max(rows))
    scale = 1.8 / bound
    x = scale * cfast(adjoint, 2.0 * one - scale * gram)
    for _ in range(boosts):
        x = BOOST * x
        x = cfast(x, 2.0 * one - cfast(high, x))
    x_ref[...] = x

    def gap_of(x):
        xh, xl = halves(x)
        sh, sl = spread(xh), spread(xl)
        return one - (dot(high, sh) + (dot(high, sl) + dot(low, sh)))

    def fast(carry):
        count, _ = carry
        x = x_ref[...]
        gap = one - cfast(high, x)
        x_ref[...] = cfast(x, one + gap)
        return count + 1, total(gap * gap)

    def slow(carry):
        count, _ = carry
        x = x_ref[...]
        gap = gap_of(x)
        x_ref[...] = cdot(x, one + gap, dot_three)
        return count + 1, total(gap * gap)

    def refine(carry):
        count, _ = carry
        x = x_ref[...]
        gap = gap_of(x)
        x_ref[...] = x + cfast(x, gap)
        return count + 1, total(gap * gap)

    state = (jnp.int32(0), jnp.float32(1e30))
    state = lax.while_loop(lambda c: (c[0] < FAST_STEPS) & (c[1] > 1.0), fast, state)
    state = lax.while_loop(lambda c: (c[0] < FULL_STEPS) & (c[1] > 1.0), slow, state)
    state = (state[0], jnp.float32(1e30))
    lax.while_loop(lambda c: (c[0] < 2 * FULL_STEPS) & (c[1] > 1e-4), refine, state)
    return x_ref[...]


def block_of(b, row, column):
    n = b.shape[1] // 2
    part = b[row * FACE:(row + 1) * FACE]
    at = column * FACE
    return jnp.concatenate([part[:, at:at + FACE], part[:, n + at:n + at + FACE]], axis=1)


def times_real(x, y):
    m = x.shape[1] // 2
    both = dot_three(jnp.concatenate([x[:, :m], x[:, m:]], axis=0), y)
    n = x.shape[0]
    return jnp.concatenate([both[:n], both[n:]], axis=1)


def setup_kernel(
    blocks_ref, mask_ref, last_ref, energy_ref, modes_ref, levels_ref, coupling_ref,
    link_ref, v_ref, b_ref, w_ref, inner_ref, arm_ref, const_ref,
):
    for number in range(2 * NB):
        start = pl.multiple_of(blocks_ref[number] * BLOCK, BLOCK)
        v_ref[number * BLOCK:(number + 1) * BLOCK, :] = modes_ref[pl.ds(start, BLOCK), :]
    detuning = energy_ref[0] - levels_ref[...]
    denominator = detuning * detuning + broadening * broadening
    real, imag = detuning / denominator, -broadening / denominator
    w_ref[...] = jnp.concatenate([real, imag], axis=0)
    v = v_ref[...]
    n = v.shape[0]
    both = dot_three(jnp.concatenate([v * real, v * imag], axis=0), v, NT)
    b_ref[...] = jnp.concatenate([both[:n], both[n:]], axis=1)
    b = b_ref[...]
    ll, lr = block_of(b, 0, 0), block_of(b, 0, 1)
    rl, rr = block_of(b, 1, 0), block_of(b, 1, 1)
    rows = lax.broadcasted_iota(jnp.int32, (FACE, FACE), 0)
    columns = lax.broadcasted_iota(jnp.int32, (FACE, FACE), 1)
    ones = [[mask_ref[i, j].astype(f32) for j in range(NB)] for i in range(NB)]
    upper = jnp.where(columns < BLOCK, ones[0][0], ones[0][1])
    lower = jnp.where(columns < BLOCK, ones[1][0], ones[1][1])
    masked = coupling_ref[...] * jnp.where(rows < BLOCK, upper, lower)
    link = jnp.where(last_ref[0] == 1, jnp.where(rows == columns, 1.0, 0.0), masked)
    link_ref[...] = link
    coupled = times_real(dot_three(link.T, rr), link)
    inner_ref[0] = ll
    inner_ref[1] = coupled
    arm_ref[0] = dot_three(link.T, rl)
    arm_ref[1] = times_real(lr, link)
    const_ref[0] = coupled
    const_ref[1] = ll


def contact_sigma():
    rows = lax.broadcasted_iota(jnp.int32, (FACE, 2 * FACE), 0)
    columns = lax.broadcasted_iota(jnp.int32, (FACE, 2 * FACE), 1)
    return jnp.where(columns == rows + FACE, -contact_rate, 0.0).astype(f32)


def initial_kernel(meta_ref, inner_ref, arm_ref, const_ref, out_ref, x_ref):
    one_step(0, meta_ref, contact_sigma, inner_ref, arm_ref, const_ref, out_ref, x_ref)


def step_kernel(meta_ref, sigma_ref, inner_ref, arm_ref, const_ref, out_ref, x_ref):
    one_step(2, meta_ref, lambda: sigma_ref[...], inner_ref, arm_ref, const_ref, out_ref, x_ref)


def one_step(boosts, meta_ref, sigma_of, inner_ref, arm_ref, const_ref, out_ref, x_ref):
    way = meta_ref[1]

    @pl.when(meta_ref[0] == 1)
    def _():
        sigma = sigma_of()
        arm = arm_ref[way]
        a = unit(FACE) - cdot(inner_ref[way], sigma, dot_three)
        early = cdot(arm, sigma, dot_three)
        x = inverse(a, x_ref, boosts)
        out_ref[...] = const_ref[way] + cdot(cdot(early, x, dot_three), turned(arm, 1.0), dot_three)


MESH = pl.DeviceIdType.MESH


class Hop:
    def __init__(self, t, out_ref, in_ref, sent, came):
        here, slabs = lax.axis_index("slab"), lax.axis_size("slab")
        self.sides = []
        for side, (start, end) in enumerate(((t, t + 1), (slabs - 1 - t, slabs - 2 - t))):
            copy = pltpu.make_async_remote_copy(
                out_ref, in_ref, sent.at[side], came.at[side],
                device_id={"slab": end}, device_id_type=MESH,
            )
            self.sides.append((here == start, here == end, start, copy))

    def greet(self, barrier):
        for _, receives, start, _ in self.sides:
            @pl.when(receives)
            def _():
                pl.semaphore_signal(barrier, inc=1, device_id={"slab": start}, device_id_type=MESH)

    def expected(self):
        return sum(sends.astype(jnp.int32) for sends, _, _, _ in self.sides)

    def start(self):
        for sends, _, _, copy in self.sides:
            @pl.when(sends)
            def _():
                copy.start()

    def wait(self):
        for sends, receives, _, copy in self.sides:
            @pl.when(sends)
            def _():
                copy.wait_send()

            @pl.when(receives)
            def _():
                copy.wait_recv()


class Halo:
    def __init__(self, own_ref, above_ref, below_ref, first, count, sent, came):
        here, energies = lax.axis_index("energy"), lax.axis_size("energy")
        self.has_above, self.has_below = here < energies - 1, here > 0
        self.up, self.down = {"energy": here + 1}, {"energy": here - 1}
        rows = pl.ds(first, count)
        own = own_ref.at[:, rows, :]
        self.to_above = pltpu.make_async_remote_copy(
            own, below_ref, sent.at[0], came.at[0], device_id=self.up, device_id_type=MESH
        )
        self.to_below = pltpu.make_async_remote_copy(
            own, above_ref, sent.at[1], came.at[1], device_id=self.down, device_id_type=MESH
        )
        self.landing = (above_ref, below_ref)

    def greet(self, barrier):
        for there, device in ((self.has_above, self.up), (self.has_below, self.down)):
            @pl.when(there)
            def _():
                pl.semaphore_signal(barrier, inc=1, device_id=device, device_id_type=MESH)

    def expected(self):
        return self.has_above.astype(jnp.int32) + self.has_below.astype(jnp.int32)

    def start(self):
        above_ref, below_ref = self.landing

        @pl.when(self.has_above)
        def _():
            self.to_above.start()

        @pl.when(self.has_below)
        def _():
            self.to_below.start()

        @pl.when(jnp.logical_not(self.has_below))
        def _():
            below_ref[...] = jnp.zeros_like(below_ref)

        @pl.when(jnp.logical_not(self.has_above))
        def _():
            above_ref[...] = jnp.zeros_like(above_ref)

    def wait(self):
        @pl.when(self.has_below)
        def _():
            self.to_above.wait_recv()
            self.to_below.wait_send()

        @pl.when(self.has_above)
        def _():
            self.to_below.wait_recv()
            self.to_above.wait_send()


def open_all(parts):
    barrier = pltpu.get_barrier_semaphore()
    for part in parts:
        part.greet(barrier)
    expected = sum(part.expected() for part in parts)

    @pl.when(expected > 0)
    def _():
        pl.semaphore_wait(barrier, expected)


EARLY_ROWS = 192


def first_hop(t, out_ref, own_ref, in_ref, above_ref, below_ref, s0, c0, s1, c1):
    hop = Hop(t, out_ref, in_ref, s0, c0)
    halo = Halo(own_ref, above_ref, below_ref, 0, EARLY_ROWS, s1, c1)
    open_all([hop, halo])
    hop.start()
    halo.start()
    halo.wait()
    hop.wait()


def middle_hop(t, out_ref, in_ref, s0, c0):
    hop = Hop(t, out_ref, in_ref, s0, c0)
    open_all([hop])
    hop.start()
    hop.wait()


def last_hop(
    t, shift_ref, out_ref, own_ref, b_ref, above_ref, below_ref,
    in_ref, mix_ref, part_ref, above_rest, below_rest, s0, c0, s1, c1,
):
    n = own_ref.shape[1]
    hop = Hop(t, out_ref, in_ref, s0, c0)
    halo = Halo(own_ref, above_rest, below_rest, EARLY_ROWS, n - EARLY_ROWS, s1, c1)
    open_all([hop, halo])
    hop.start()
    halo.start()
    shifted = shift_ref[0] != 0

    def mix_rows(rows, above, below):
        for part in range(2):
            own = own_ref[part, rows, :]
            around = jnp.where(shifted, above[part] + below[part], own + own)
            mix_ref[rows, part * n:(part + 1) * n] = phonon_strength * around

    mix_rows(slice(0, EARLY_ROWS), above_ref, below_ref)
    halo.wait()
    mix_rows(slice(EARLY_ROWS, n), above_rest, below_rest)
    part_ref[...] = unit(n) - cdot(b_ref[...], mix_ref[...], dot_three)
    hop.wait()


def final_kernel(meta_ref, link_ref, b_ref, v_ref, w_ref, mix_ref, part_ref, *rest):
    *incoming, out_ref, a_ref, s_ref, x_ref = rest
    slabs = len(incoming) + 1
    position = meta_ref[2]
    contact = contact_sigma()
    left = jnp.where(position == 0, contact, 0.0)
    right = jnp.where(position == slabs - 1, contact, 0.0)
    for t, piece in enumerate(incoming):
        value = piece[...]
        left = jnp.where(position == t + 1, value, left)
        right = jnp.where(position == slabs - 2 - t, value, right)
    link = link_ref[...]
    right = times_real(dot_three(link, right), link.T)
    n = b_ref.shape[0]
    b = b_ref[...]
    for at, sigma in ((0, left), (FACE, right)):
        columns_of_b = jnp.concatenate([b[:, at:at + FACE], b[:, n + at:n + at + FACE]], axis=1)
        change = cdot(columns_of_b, sigma, dot_three)
        for part in range(2):
            lanes = slice(part * n + at, part * n + at + FACE)
            a_ref[:, lanes] = part_ref[:, lanes] - change[:, part * FACE:(part + 1) * FACE]
            s_ref[:, lanes] = mix_ref[:, lanes]
            s_ref[at:at + FACE, lanes] += sigma[:, part * FACE:(part + 1) * FACE]
    v = v_ref[...]
    s = s_ref[...]
    before = dot_three(s, v, TN)
    x = inverse(a_ref[...], x_ref, 3)
    after = dot_three(jnp.concatenate([x[:, :n], x[:, n:]], axis=0), v)
    sr, si, xr, xi = before[:n], before[n:], after[:n], after[n:]
    dr = jnp.sum(sr * xr - si * xi, axis=0, keepdims=True)
    di = jnp.sum(sr * xi + si * xr, axis=0, keepdims=True)
    wr, wi = w_ref[0:1, :], w_ref[1:2, :]
    qr, qi = wr * wr - wi * wi, 2.0 * wr * wi
    out_ref[0, 0] = wr + qr * dr - qi * di
    out_ref[1, 0] = wi + qr * di + qi * dr


VM = pl.BlockSpec(memory_space=pltpu.VMEM)
SM = pl.BlockSpec(memory_space=pltpu.SMEM)


def call(kernel, outs, in_specs, scratch=(), channel=None):
    shapes = [jax.ShapeDtypeStruct(shape, f32) for shape in outs]
    return pl.pallas_call(
        kernel,
        out_shape=shapes,
        in_specs=in_specs,
        out_specs=[VM] * len(outs),
        scratch_shapes=[pltpu.VMEM(x, f32) if isinstance(x, tuple) else x for x in scratch],
        compiler_params=pltpu.CompilerParams(
            vmem_limit_bytes=48 * 1024 * 1024,
            collective_id=channel,
            has_side_effects=channel is not None,
        ),
    )


def body(slab_modes, levels, boundary_blocks, coupling_mask, coupling, phonon_shift, prev_green):
    assert prev_green.shape[2] == 1
    slabs = lax.axis_size("slab")
    energies = lax.axis_size("energy")
    assert slabs % 2 == 0
    position = lax.axis_index("slab")
    grid_index = lax.axis_index("energy")
    energy = energy_low + energy_span * (grid_index.astype(f32) + 0.5) / energies
    n = 2 * FACE
    orbitals = slab_modes.shape[2]

    pair = (2, FACE, 2 * FACE)
    last = (position == slabs - 1).astype(jnp.int32)[None]
    link, v, b, w, inner, arm, const = call(
        setup_kernel,
        [(FACE, FACE), (n, orbitals), (n, 2 * n), (2, orbitals), pair, pair, pair],
        [SM] * 4 + [VM] * 3,
    )(
        boundary_blocks[0], coupling_mask[0], last, energy[None],
        slab_modes[0], levels, coupling[0],
    )

    sigma = mix = part = None
    incoming = []
    own = prev_green[:, 0, 0]
    early = (2, EARLY_ROWS, n)
    rest = pltpu.VMEM((2, n - EARLY_ROWS, n), f32)
    two = pltpu.SemaphoreType.DMA((2,))
    assert slabs >= 4
    for t in range(slabs - 1):
        active = (position == t) | (position == slabs - 1 - t)
        way = jnp.where(position == t, 0, 1)
        meta = jnp.stack([active.astype(jnp.int32), way.astype(jnp.int32), position])
        kernel, given = (step_kernel, (sigma,)) if t else (initial_kernel, ())
        (outgoing,) = call(kernel, [pair[1:]], [SM] + [VM] * (3 + len(given)), [pair[1:]])(
            meta, *given, inner, arm, const
        )
        if t == 0:
            sigma, above, below = call(
                functools.partial(first_hop, t), [pair[1:], early, early], [VM] * 2,
                [two] * 4, t,
            )(outgoing, own)
        elif t < slabs - 2:
            (sigma,) = call(
                functools.partial(middle_hop, t), [pair[1:]], [VM], [two] * 2, t
            )(outgoing)
        else:
            sigma, mix, part = call(
                functools.partial(last_hop, t), [pair[1:], (n, 2 * n), (n, 2 * n)],
                [SM] + [VM] * 5, [rest, rest] + [two] * 4, t,
            )(phonon_shift, outgoing, own, b, above, below)
        incoming.append(sigma)
    (result,) = call(
        final_kernel, [(2, 1, 1, orbitals)], [SM] + [VM] * (6 + slabs - 1), [(n, 2 * n)] * 3
    )(meta, link, b, v, w, mix, part, *incoming)
    return result


def solution(mesh):
    in_specs = (
        P("slab", None, None),
        P("slab", None),
        P("slab", None),
        P("slab", None, None),
        P("slab", None, None),
        P("slab"),
        P(None, "slab", "energy", None, None),
    )
    out_specs = P(None, "slab", "energy", None)
    return jax.shard_map(body, mesh=mesh, in_specs=in_specs, out_specs=out_specs, check_vma=False)
```

```python
import functools

import jax
import jax.numpy as jnp
from jax import lax
from jax.experimental import pallas as pl
from jax.experimental.pallas import tpu as pltpu
from jax.sharding import PartitionSpec as P

BLOCK = 64
NB = 2
FACE = BLOCK * NB

broadening = 0.2
contact_rate = 0.2
phonon_strength = 0.03
energy_low = -2.5
energy_span = 5.0

NN = (((1,), (0,)), ((), ()))
NT = (((1,), (1,)), ((), ()))
TN = (((0,), (0,)), ((), ()))
f32 = jnp.float32
bf16 = jnp.bfloat16


def dot_fast(a, b, dims=NN):
    return lax.dot_general(a.astype(bf16), b.astype(bf16), dims, preferred_element_type=f32)


def halves(a):
    high = a.astype(bf16)
    return high, (a - high.astype(f32)).astype(bf16)


def dot_three(a, b, dims=NN):
    ah, al = halves(a)
    bh, bl = halves(b)
    dot = functools.partial(lax.dot_general, dimension_numbers=dims, preferred_element_type=f32)
    return dot(ah, bh) + (dot(ah, bl) + dot(al, bh))


def spread(y):
    m = y.shape[1] // 2
    real, imag = y[:, :m], y[:, m:]
    return jnp.concatenate(
        [jnp.concatenate([real, imag], axis=1), jnp.concatenate([-imag, real], axis=1)], axis=0
    )


def cdot(x, y, dot):
    return dot(x, spread(y))


def turned(y, sign):
    m = y.shape[1] // 2
    return jnp.concatenate([y[:, :m].T, sign * y[:, m:].T], axis=1)


def unit(n):
    rows = lax.broadcasted_iota(jnp.int32, (n, 2 * n), 0)
    columns = lax.broadcasted_iota(jnp.int32, (n, 2 * n), 1)
    return jnp.where(rows == columns, 1.0, 0.0).astype(f32)


def total(x):
    return jnp.sum(jnp.sum(x, axis=0, keepdims=True), axis=1, keepdims=True)[0, 0]


BOOST = 1.85
FAST_STEPS = 14
FULL_STEPS = 40


def inverse(a, x_ref, boosts):
    n = a.shape[0]
    one = unit(n)
    adjoint = turned(a, -1.0)
    high, low = halves(a)
    dot = functools.partial(lax.dot_general, dimension_numbers=NN, preferred_element_type=f32)

    def cfast(x, y):
        return dot(x.astype(bf16), spread(y.astype(bf16)))

    gram = cfast(high, adjoint)
    frobenius = jnp.sqrt(total(gram * gram))
    rows = jnp.sum(jnp.abs(gram), axis=1, keepdims=True)
    bound = jnp.minimum(frobenius, jnp.max(rows))
    scale = 1.8 / bound
    x = scale * cfast(adjoint, 2.0 * one - scale * gram)
    for _ in range(boosts):
        x = BOOST * x
        x = cfast(x, 2.0 * one - cfast(high, x))
    x_ref[...] = x

    def gap_of(x):
        xh, xl = halves(x)
        sh, sl = spread(xh), spread(xl)
        return one - (dot(high, sh) + (dot(high, sl) + dot(low, sh)))

    def fast(carry):
        count, _ = carry
        x = x_ref[...]
        gap = one - cfast(high, x)
        x_ref[...] = cfast(x, one + gap)
        return count + 1, total(gap * gap)

    def slow(carry):
        count, _ = carry
        x = x_ref[...]
        gap = gap_of(x)
        x_ref[...] = cdot(x, one + gap, dot_three)
        return count + 1, total(gap * gap)

    def refine(carry):
        count, _ = carry
        x = x_ref[...]
        gap = gap_of(x)
        x_ref[...] = x + cfast(x, gap)
        return count + 1, total(gap * gap)

    state = (jnp.int32(0), jnp.float32(1e30))
    state = lax.while_loop(lambda c: (c[0] < FAST_STEPS) & (c[1] > 1.0), fast, state)
    state = lax.while_loop(lambda c: (c[0] < FULL_STEPS) & (c[1] > 1.0), slow, state)
    state = (state[0], jnp.float32(1e30))
    lax.while_loop(lambda c: (c[0] < 2 * FULL_STEPS) & (c[1] > 1e-4), refine, state)
    return x_ref[...]


def block_of(b, row, column):
    n = b.shape[1] // 2
    part = b[row * FACE:(row + 1) * FACE]
    at = column * FACE
    return jnp.concatenate([part[:, at:at + FACE], part[:, n + at:n + at + FACE]], axis=1)


def times_real(x, y):
    m = x.shape[1] // 2
    both = dot_three(jnp.concatenate([x[:, :m], x[:, m:]], axis=0), y)
    n = x.shape[0]
    return jnp.concatenate([both[:n], both[n:]], axis=1)


def setup_kernel(
    blocks_ref, mask_ref, last_ref, energy_ref, modes_ref, levels_ref, coupling_ref,
    link_ref, v_ref, b_ref, w_ref, inner_ref, arm_ref, const_ref,
):
    for number in range(2 * NB):
        start = pl.multiple_of(blocks_ref[number] * BLOCK, BLOCK)
        v_ref[number * BLOCK:(number + 1) * BLOCK, :] = modes_ref[pl.ds(start, BLOCK), :]
    detuning = energy_ref[0] - levels_ref[...]
    denominator = detuning * detuning + broadening * broadening
    real, imag = detuning / denominator, -broadening / denominator
    w_ref[...] = jnp.concatenate([real, imag], axis=0)
    v = v_ref[...]
    n = v.shape[0]
    both = dot_three(jnp.concatenate([v * real, v * imag], axis=0), v, NT)
    b_ref[...] = jnp.concatenate([both[:n], both[n:]], axis=1)
    b = b_ref[...]
    ll, lr = block_of(b, 0, 0), block_of(b, 0, 1)
    rl, rr = block_of(b, 1, 0), block_of(b, 1, 1)
    rows = lax.broadcasted_iota(jnp.int32, (FACE, FACE), 0)
    columns = lax.broadcasted_iota(jnp.int32, (FACE, FACE), 1)
    ones = [[mask_ref[i, j].astype(f32) for j in range(NB)] for i in range(NB)]
    upper = jnp.where(columns < BLOCK, ones[0][0], ones[0][1])
    lower = jnp.where(columns < BLOCK, ones[1][0], ones[1][1])
    masked = coupling_ref[...] * jnp.where(rows < BLOCK, upper, lower)
    link = jnp.where(last_ref[0] == 1, jnp.where(rows == columns, 1.0, 0.0), masked)
    link_ref[...] = link
    coupled = times_real(dot_three(link.T, rr), link)
    inner_ref[0] = ll
    inner_ref[1] = coupled
    arm_ref[0] = dot_three(link.T, rl)
    arm_ref[1] = times_real(lr, link)
    const_ref[0] = coupled
    const_ref[1] = ll


def contact_sigma():
    rows = lax.broadcasted_iota(jnp.int32, (FACE, 2 * FACE), 0)
    columns = lax.broadcasted_iota(jnp.int32, (FACE, 2 * FACE), 1)
    return jnp.where(columns == rows + FACE, -contact_rate, 0.0).astype(f32)


def initial_kernel(meta_ref, inner_ref, arm_ref, const_ref, out_ref, x_ref):
    one_step(0, meta_ref, contact_sigma, inner_ref, arm_ref, const_ref, out_ref, x_ref)


def step_kernel(meta_ref, sigma_ref, inner_ref, arm_ref, const_ref, out_ref, x_ref):
    one_step(2, meta_ref, lambda: sigma_ref[...], inner_ref, arm_ref, const_ref, out_ref, x_ref)


def one_step(boosts, meta_ref, sigma_of, inner_ref, arm_ref, const_ref, out_ref, x_ref):
    way = meta_ref[1]

    @pl.when(meta_ref[0] == 1)
    def _():
        sigma = sigma_of()
        arm = arm_ref[way]
        a = unit(FACE) - cdot(inner_ref[way], sigma, dot_three)
        early = cdot(arm, sigma, dot_three)
        x = inverse(a, x_ref, boosts)
        out_ref[...] = const_ref[way] + cdot(cdot(early, x, dot_three), turned(arm, 1.0), dot_three)


MESH = pl.DeviceIdType.MESH


class Hop:
    def __init__(self, t, out_ref, in_ref, sent, came):
        here, slabs = lax.axis_index("slab"), lax.axis_size("slab")
        self.sides = []
        for side, (start, end) in enumerate(((t, t + 1), (slabs - 1 - t, slabs - 2 - t))):
            copy = pltpu.make_async_remote_copy(
                out_ref, in_ref, sent.at[side], came.at[side],
                device_id={"slab": end}, device_id_type=MESH,
            )
            self.sides.append((here == start, here == end, start, copy))

    def greet(self, barrier):
        for _, receives, start, _ in self.sides:
            @pl.when(receives)
            def _():
                pl.semaphore_signal(barrier, inc=1, device_id={"slab": start}, device_id_type=MESH)

    def expected(self):
        return sum(sends.astype(jnp.int32) for sends, _, _, _ in self.sides)

    def start(self):
        for sends, _, _, copy in self.sides:
            @pl.when(sends)
            def _():
                copy.start()

    def wait(self):
        for sends, receives, _, copy in self.sides:
            @pl.when(sends)
            def _():
                copy.wait_send()

            @pl.when(receives)
            def _():
                copy.wait_recv()


class Halo:
    def __init__(self, own_ref, above_ref, below_ref, first, count, sent, came):
        here, energies = lax.axis_index("energy"), lax.axis_size("energy")
        self.has_above, self.has_below = here < energies - 1, here > 0
        self.up, self.down = {"energy": here + 1}, {"energy": here - 1}
        rows = pl.ds(first, count)
        own = own_ref.at[:, rows, :]
        self.to_above = pltpu.make_async_remote_copy(
            own, below_ref, sent.at[0], came.at[0], device_id=self.up, device_id_type=MESH
        )
        self.to_below = pltpu.make_async_remote_copy(
            own, above_ref, sent.at[1], came.at[1], device_id=self.down, device_id_type=MESH
        )
        self.landing = (above_ref, below_ref)

    def greet(self, barrier):
        for there, device in ((self.has_above, self.up), (self.has_below, self.down)):
            @pl.when(there)
            def _():
                pl.semaphore_signal(barrier, inc=1, device_id=device, device_id_type=MESH)

    def expected(self):
        return self.has_above.astype(jnp.int32) + self.has_below.astype(jnp.int32)

    def start(self):
        above_ref, below_ref = self.landing

        @pl.when(self.has_above)
        def _():
            self.to_above.start()

        @pl.when(self.has_below)
        def _():
            self.to_below.start()

        @pl.when(jnp.logical_not(self.has_below))
        def _():
            below_ref[...] = jnp.zeros_like(below_ref)

        @pl.when(jnp.logical_not(self.has_above))
        def _():
            above_ref[...] = jnp.zeros_like(above_ref)

    def wait(self):
        @pl.when(self.has_below)
        def _():
            self.to_above.wait_recv()
            self.to_below.wait_send()

        @pl.when(self.has_above)
        def _():
            self.to_below.wait_recv()
            self.to_above.wait_send()


def open_all(parts):
    barrier = pltpu.get_barrier_semaphore()
    for part in parts:
        part.greet(barrier)
    expected = sum(part.expected() for part in parts)

    @pl.when(expected > 0)
    def _():
        pl.semaphore_wait(barrier, expected)


EARLY_ROWS = 128
MIDDLE_ROWS = 64


def first_hop(t, out_ref, own_ref, in_ref, above_ref, below_ref, s0, c0, s1, c1):
    hop = Hop(t, out_ref, in_ref, s0, c0)
    halo = Halo(own_ref, above_ref, below_ref, 0, EARLY_ROWS, s1, c1)
    open_all([hop, halo])
    hop.start()
    halo.start()
    halo.wait()
    hop.wait()


def middle_hop(t, out_ref, in_ref, s0, c0):
    hop = Hop(t, out_ref, in_ref, s0, c0)
    open_all([hop])
    hop.start()
    hop.wait()


def second_hop(t, out_ref, own_ref, in_ref, above_ref, below_ref, s0, c0, s1, c1):
    hop = Hop(t, out_ref, in_ref, s0, c0)
    halo = Halo(own_ref, above_ref, below_ref, EARLY_ROWS, MIDDLE_ROWS, s1, c1)
    open_all([hop, halo])
    hop.start()
    halo.start()
    hop.wait()
    halo.wait()


def last_hop(
    t, shift_ref, out_ref, own_ref, b_ref, above_ref, below_ref, above_mid, below_mid,
    in_ref, mix_ref, part_ref, above_rest, below_rest, s0, c0, s1, c1,
):
    n = own_ref.shape[1]
    late = EARLY_ROWS + MIDDLE_ROWS
    hop = Hop(t, out_ref, in_ref, s0, c0)
    halo = Halo(own_ref, above_rest, below_rest, late, n - late, s1, c1)
    open_all([hop, halo])
    hop.start()
    halo.start()
    shifted = shift_ref[0] != 0

    def mix_rows(rows, above, below):
        for part in range(2):
            own = own_ref[part, rows, :]
            around = jnp.where(shifted, above[part] + below[part], own + own)
            mix_ref[rows, part * n:(part + 1) * n] = phonon_strength * around

    mix_rows(slice(0, EARLY_ROWS), above_ref, below_ref)
    mix_rows(slice(EARLY_ROWS, late), above_mid, below_mid)
    halo.wait()
    mix_rows(slice(late, n), above_rest, below_rest)
    part_ref[...] = unit(n) - cdot(b_ref[...], mix_ref[...], dot_three)
    hop.wait()


def final_kernel(meta_ref, link_ref, b_ref, v_ref, w_ref, mix_ref, part_ref, *rest):
    *incoming, out_ref, a_ref, s_ref, x_ref = rest
    slabs = len(incoming) + 1
    position = meta_ref[2]
    contact = contact_sigma()
    left = jnp.where(position == 0, contact, 0.0)
    right = jnp.where(position == slabs - 1, contact, 0.0)
    for t, piece in enumerate(incoming):
        value = piece[...]
        left = jnp.where(position == t + 1, value, left)
        right = jnp.where(position == slabs - 2 - t, value, right)
    link = link_ref[...]
    right = times_real(dot_three(link, right), link.T)
    n = b_ref.shape[0]
    b = b_ref[...]
    for at, sigma in ((0, left), (FACE, right)):
        columns_of_b = jnp.concatenate([b[:, at:at + FACE], b[:, n + at:n + at + FACE]], axis=1)
        change = cdot(columns_of_b, sigma, dot_three)
        for part in range(2):
            lanes = slice(part * n + at, part * n + at + FACE)
            a_ref[:, lanes] = part_ref[:, lanes] - change[:, part * FACE:(part + 1) * FACE]
            s_ref[:, lanes] = mix_ref[:, lanes]
            s_ref[at:at + FACE, lanes] += sigma[:, part * FACE:(part + 1) * FACE]
    v = v_ref[...]
    s = s_ref[...]
    before = dot_three(s, v, TN)
    x = inverse(a_ref[...], x_ref, 3)
    after = dot_three(jnp.concatenate([x[:, :n], x[:, n:]], axis=0), v)
    sr, si, xr, xi = before[:n], before[n:], after[:n], after[n:]
    dr = jnp.sum(sr * xr - si * xi, axis=0, keepdims=True)
    di = jnp.sum(sr * xi + si * xr, axis=0, keepdims=True)
    wr, wi = w_ref[0:1, :], w_ref[1:2, :]
    qr, qi = wr * wr - wi * wi, 2.0 * wr * wi
    out_ref[0, 0] = wr + qr * dr - qi * di
    out_ref[1, 0] = wi + qr * di + qi * dr


VM = pl.BlockSpec(memory_space=pltpu.VMEM)
SM = pl.BlockSpec(memory_space=pltpu.SMEM)


def call(kernel, outs, in_specs, scratch=(), channel=None):
    shapes = [jax.ShapeDtypeStruct(shape, f32) for shape in outs]
    return pl.pallas_call(
        kernel,
        out_shape=shapes,
        in_specs=in_specs,
        out_specs=[VM] * len(outs),
        scratch_shapes=[pltpu.VMEM(x, f32) if isinstance(x, tuple) else x for x in scratch],
        compiler_params=pltpu.CompilerParams(
            vmem_limit_bytes=48 * 1024 * 1024,
            collective_id=channel,
            has_side_effects=channel is not None,
        ),
    )


def body(slab_modes, levels, boundary_blocks, coupling_mask, coupling, phonon_shift, prev_green):
    assert prev_green.shape[2] == 1
    slabs = lax.axis_size("slab")
    energies = lax.axis_size("energy")
    assert slabs % 2 == 0
    position = lax.axis_index("slab")
    grid_index = lax.axis_index("energy")
    energy = energy_low + energy_span * (grid_index.astype(f32) + 0.5) / energies
    n = 2 * FACE
    orbitals = slab_modes.shape[2]

    pair = (2, FACE, 2 * FACE)
    last = (position == slabs - 1).astype(jnp.int32)[None]
    link, v, b, w, inner, arm, const = call(
        setup_kernel,
        [(FACE, FACE), (n, orbitals), (n, 2 * n), (2, orbitals), pair, pair, pair],
        [SM] * 4 + [VM] * 3,
    )(
        boundary_blocks[0], coupling_mask[0], last, energy[None],
        slab_modes[0], levels, coupling[0],
    )

    sigma = mix = part = None
    incoming = []
    own = prev_green[:, 0, 0]
    early = (2, EARLY_ROWS, n)
    rest = pltpu.VMEM((2, n - EARLY_ROWS - MIDDLE_ROWS, n), f32)
    two = pltpu.SemaphoreType.DMA((2,))
    assert slabs >= 4
    for t in range(slabs - 1):
        active = (position == t) | (position == slabs - 1 - t)
        way = jnp.where(position == t, 0, 1)
        meta = jnp.stack([active.astype(jnp.int32), way.astype(jnp.int32), position])
        kernel, given = (step_kernel, (sigma,)) if t else (initial_kernel, ())
        (outgoing,) = call(kernel, [pair[1:]], [SM] + [VM] * (3 + len(given)), [pair[1:]])(
            meta, *given, inner, arm, const
        )
        if t == 0:
            sigma, above, below = call(
                functools.partial(first_hop, t), [pair[1:], early, early], [VM] * 2,
                [two] * 4, t,
            )(outgoing, own)
        elif t == 1:
            middle = (2, MIDDLE_ROWS, n)
            sigma, above_mid, below_mid = call(
                functools.partial(second_hop, t), [pair[1:], middle, middle], [VM] * 2,
                [two] * 4, t,
            )(outgoing, own)
        elif t < slabs - 2:
            (sigma,) = call(
                functools.partial(middle_hop, t), [pair[1:]], [VM], [two] * 2, t
            )(outgoing)
        else:
            sigma, mix, part = call(
                functools.partial(last_hop, t), [pair[1:], (n, 2 * n), (n, 2 * n)],
                [SM] + [VM] * 7, [rest, rest] + [two] * 4, t,
            )(phonon_shift, outgoing, own, b, above, below, above_mid, below_mid)
        incoming.append(sigma)
    (result,) = call(
        final_kernel, [(2, 1, 1, orbitals)], [SM] + [VM] * (6 + slabs - 1), [(n, 2 * n)] * 3
    )(meta, link, b, v, w, mix, part, *incoming)
    return result


def solution(mesh):
    in_specs = (
        P("slab", None, None),
        P("slab", None),
        P("slab", None),
        P("slab", None, None),
        P("slab", None, None),
        P("slab"),
        P(None, "slab", "energy", None, None),
    )
    out_specs = P(None, "slab", "energy", None)
    return jax.shard_map(body, mesh=mesh, in_specs=in_specs, out_specs=out_specs, check_vma=False)
```
